32 devices in a mesh: sweep: 4 (over z), cross: 2 (over y), third: 4 (over x, core).
Axes of the slice: x: 2, y: 2, z: 4, core: 2. Of those that a mesh axis runs over, the one named last changes fastest.
Arguments:
- rhs: float32 [32, 32, 64, 128], P('sweep', 'cross', 'third'), may hold values from -6 to 6
- guess: float32 [32, 32, 64, 128], P('sweep', 'cross', 'third'), may hold values from -6 to 6
- inv_diag: float32 [128, 128], replicated, may hold values from -0.25 to 1.25
- face_mats: float32 [6, 32, 128], replicated, may hold values from -0.4375 to 0.4375
- extract: float32 [4, 128, 32], replicated, may hold values from -0.5 to 0.5
- lift: float32 [32, 96], replicated, may hold values from -1 to 1
- transport: float32 [32, 32], P('sweep'), may hold values from 0 to 1, as said below
- boundary: float32 [32, 64, 32], P('cross', 'third'), may hold values from -6 to 6
- scale_index: int32 [32, 32, 64], P('sweep', 'cross', 'third'), may hold values from 0 to 3
- wind: int32 [2, 32, 32, 64], P(None, 'sweep', 'cross', 'third'), may hold values from 0 to 1
Outputs:
- solution: float32 [32, 32, 64, 128], P('sweep', 'cross', 'third')
The draws below stay inside these ranges and needn't reach their ends.
Inputs may be any that keep to these rules, and one draw needn't show every extreme that they name: `transport`: transmission factors are positive.
All inputs are finite; a program needn't handle non-finite values.
Results may differ from the reference program's by a relative error of at most 0.0003.
Values sent between devices are 32-bit elements; how exact they have to be, the bound alone decides.
A program may use at most 64 MiB of HBM per device.

```python
import jax
import jax.numpy as jnp
from jax import lax

DOF = 128
TRACE = 32
SWEEPS = 2
WIND_PLANE_COUNT = 32
NY = 32
NZ = 64


def draw_inv_diag(key, part):
    first, second_piece = jax.random.split(key, 2)
    offdiag = jnp.clip(jax.random.normal(first, (DOF, DOF), jnp.float32), -4.0, 4.0) * 0.06
    diagonal = jax.random.uniform(second_piece, (DOF,), jnp.float32, 0.6, 1.0)
    return offdiag * (1.0 - jnp.eye(DOF, dtype=jnp.float32)) + jnp.eye(DOF, dtype=jnp.float32) * diagonal[None, :]


def draw_transport(key, part):
    random_keys = jax.random.split(key, 5)
    share = 0.5
    slow = jax.random.uniform(random_keys[0], (TRACE,)) < share
    keep = jax.random.uniform(random_keys[1], (TRACE,), jnp.float32, 0.5, 0.8)
    slow_log = jnp.log(keep) / WIND_PLANE_COUNT
    fast_log = -1.0 / jax.random.uniform(random_keys[2], (TRACE,), jnp.float32, 8.0, 16.0)
    baseline_record = jnp.where(slow, slow_log, fast_log)
    random_wobble = jax.random.uniform(random_keys[3], (WIND_PLANE_COUNT, TRACE), jnp.float32, 0.7, 1.3)
    surge_groups = jax.random.uniform(random_keys[4], (WIND_PLANE_COUNT, 1)) < 3.0 / WIND_PLANE_COUNT
    surge_record = jnp.where(surge_groups, jnp.log(0.75), 0.0)
    return jnp.exp(baseline_record[None, :] * random_wobble + surge_record)


def with_ends(entries, own_key, least, high):
    shape = entries.shape
    spot = [jax.random.randint(jax.random.fold_in(own_key, axis), (), 0, shape[axis]) for axis in range(len(shape))]
    entries = entries.at[tuple(spot)].set(least)
    longest = shape.index(max(shape))
    spot[longest] = (spot[longest] + 1) % shape[longest]
    return entries.at[tuple(spot)].set(high)


def block_levels(own_key, shape, cuts, smallest, top_value):
    level = 1.0
    for dim, parts in cuts:
        heights = jax.random.uniform(jax.random.fold_in(jax.random.fold_in(own_key, 6), dim), (parts,), jnp.float32, smallest / len(cuts), top_value / len(cuts))
        level = level * jnp.repeat(jnp.exp(heights), shape[dim] // parts).reshape((-1,) + (1,) * (len(shape) - 1 - dim))
    return level


def noise(rng, shape, scale, bound, shards=(), kind=jnp.bfloat16):
    drawn = jax.random.normal(rng, shape, jnp.float32) * scale
    if len(shards) > 0:
        drawn = block_levels(rng, shape, shards, -0.22, 0.18) * drawn
    return jnp.clip(drawn, min=-bound, max=bound).astype(kind)


def setup_inputs(seed: int = 0) -> dict:
    splits = jax.random.split(jax.random.key(seed), 11)
    return {
        "rhs": noise(splits[0], (WIND_PLANE_COUNT, NY, NZ, DOF), 1.0, 6.0, ((0, 4), (1, 2), (2, 4)), jnp.float32),
        "guess": noise(splits[1], (WIND_PLANE_COUNT, NY, NZ, DOF), 1.0, 6.0, ((0, 4), (1, 2), (2, 4)), jnp.float32),
        "inv_diag": draw_inv_diag(jax.random.fold_in(splits[10], 71), 0),
        "face_mats": noise(splits[3], (6, TRACE, DOF), (6 * TRACE) ** -0.5, 0.4375, (), jnp.float32),
        "extract": noise(splits[4], (4, DOF, TRACE), DOF ** -0.5, 0.5, (), jnp.float32),
        "lift": noise(splits[5], (TRACE, DOF - TRACE), TRACE ** -0.5, 1.0, (), jnp.float32),
        "transport": draw_transport(jax.random.fold_in(splits[10], 71), 0),
        "boundary": noise(splits[7], (NY, NZ, TRACE), 1.0, 6.0, ((0, 2), (1, 4)), jnp.float32),
        "scale_index": with_ends(jax.random.randint(splits[8], (WIND_PLANE_COUNT, NY, NZ), 0, 4), jax.random.fold_in(splits[8], 1), 0, 3).astype(jnp.int32),
        "wind": with_ends(jax.random.randint(splits[9], (2, WIND_PLANE_COUNT, NY, NZ), 0, 2), jax.random.fold_in(splits[9], 1), 0, 1).astype(jnp.int32),
    }


def product(left, right):
    return jnp.einsum("...i,ij->...j", left, right, precision=lax.Precision.HIGHEST)


def one_plane(inflow, inputs, inv_diag, faces_flat, extract, lift):
    field, rhs, diffusion, wind, transport = inputs
    padded = jnp.pad(field, ((1, 1), (1, 1), (0, 0)))
    low_y = product(padded[:-2, 1:-1], extract[0])
    high_y = product(padded[2:, 1:-1], extract[1])
    low_z = product(padded[1:-1, :-2], extract[2])
    high_z = product(padded[1:-1, 2:], extract[3])
    scaled = diffusion[..., None]
    pick_y = jnp.where(wind[0][..., None] == 1, low_y, high_y)
    pick_z = jnp.where(wind[1][..., None] == 1, low_z, high_z)
    stacked = jnp.concatenate([scaled * low_y, scaled * high_y, pick_y, scaled * low_z, scaled * high_z, pick_z], axis=-1)
    lateral = product(stacked, faces_flat)
    base = product(rhs - lateral, inv_diag) / (1.0 + scaled)
    inner = DOF - TRACE
    transmit = jnp.exp(scaled * jnp.log(transport)[None, None, :])
    outflow = transmit * inflow + base[..., inner:]
    fresh = jnp.concatenate([base[..., :inner] + product(inflow, lift), outflow], axis=-1)
    return outflow, fresh


def reference(rhs, guess, inv_diag, face_mats, extract, lift, transport, boundary, scale_index, wind):
    diffusion = 0.5 + 0.25 * scale_index.astype(jnp.float32)
    faces_flat = face_mats.reshape(6 * TRACE, DOF)
    wind_planes = jnp.moveaxis(wind, 1, 0)
    field = guess

    def step(inflow, inputs):
        return one_plane(inflow, inputs, inv_diag, faces_flat, extract, lift)

    for repeat in range(SWEEPS):
        ignored, field = lax.scan(step, boundary, (field, rhs, diffusion, wind_planes, transport))
    return field
```

```python
import functools

import jax
import jax.numpy as jnp
from jax import lax
from jax.experimental import pallas as pl
from jax.experimental.pallas import tpu as pltpu
from jax.sharding import PartitionSpec as P

SWEEPS = 2
LANES = 128
WIDTH = 32
OUT = LANES - WIDTH
f32 = jnp.float32
bf16 = jnp.bfloat16


def halves(value):
    high = value.astype(bf16)
    low = (value - high.astype(f32)).astype(bf16)
    return high, low


def doubled(weight):
    row = jnp.concatenate(halves(weight), axis=1)
    return jnp.concatenate([row, row], axis=0)


def product(left, weight):
    wide = jnp.concatenate(halves(left), axis=1)
    both = jnp.dot(wide, weight, preferred_element_type=f32)
    return both[:, :LANES] + both[:, LANES:]


def exact(left, right):
    return jnp.dot(left, right, precision=lax.Precision.HIGHEST, preferred_element_type=f32)


def turned(value, lanes):
    lanes = lanes % LANES
    return value if lanes == 0 else pltpu.roll(value, lanes, 1)


def packed(value, first):
    rows = value.shape[0] // 4
    lane = lax.broadcasted_iota(jnp.int32, (rows, LANES), 1)
    out = None
    for group in range(4):
        piece = turned(value[group * rows : (group + 1) * rows], group * WIDTH - first)
        out = piece if out is None else jnp.where(lane >= group * WIDTH, piece, out)
    return out


def unpacked(value, first):
    return jnp.concatenate([turned(value, first - group * WIDTH) for group in range(4)], axis=0)


def kernel(
    rhs_hbm, guess_hbm, inv_diag, face_mats, extract, lift, transport, boundary, scale, wind,
    out_hbm,
    rhs, guess, traces, scaled_rhs, gain_a, gain_b, mask, through, carried, ahead, base, sums,
    w_extract, w_diag, w_a, w_b, w_lift, w_lift_extract, w_ahead, lift_full, relay_gain, relay_sum,
    start, start_pair, side_out, side_in, relay_out, relay_in,
    load_sem, store_sem, side_send, side_recv, relay_send, relay_recv,
):
    planes, ny, nz, _ = rhs.shape
    cells = ny * nz
    pad = 8
    nz_all = nz + 2 * pad
    place = {axis: lax.axis_index(axis) for axis in ("sweep", "cross", "third")}
    last = {axis: lax.axis_size(axis) - 1 for axis in place}

    guess_copy = pltpu.make_async_copy(guess_hbm, guess, load_sem.at[0])
    rhs_copy = pltpu.make_async_copy(rhs_hbm, rhs, load_sem.at[1])
    guess_copy.start()
    rhs_copy.start()

    barrier = pltpu.get_barrier_semaphore()
    around = []
    for axis in place:
        around.append((axis, 1, place[axis] < last[axis]))
        around.append((axis, -1, place[axis] > 0))
    expected = jnp.int32(0)
    for axis, step, there in around:
        expected = expected + there.astype(jnp.int32)

        @pl.when(there)
        def _(axis=axis, step=step):
            pl.semaphore_signal(
                barrier, inc=1, device_id={axis: place[axis] + step},
                device_id_type=pl.DeviceIdType.MESH,
            )

    faces = ((0, "cross", 1), (1, "cross", -1), (2, "third", 1), (3, "third", -1))

    def has(axis, step):
        return place[axis] < last[axis] if step > 0 else place[axis] > 0

    def side_copy(repeat, face, axis, step):
        return pltpu.make_async_remote_copy(
            src_ref=side_out.at[repeat, face],
            dst_ref=side_in.at[repeat, face],
            send_sem=side_send.at[repeat, face],
            recv_sem=side_recv.at[repeat, face],
            device_id={axis: place[axis] + step},
            device_id_type=pl.DeviceIdType.MESH,
        )

    def relay_copy(repeat):
        return pltpu.make_async_remote_copy(
            src_ref=relay_out.at[repeat],
            dst_ref=relay_in.at[repeat],
            send_sem=relay_send.at[repeat],
            recv_sem=relay_recv.at[repeat],
            device_id={"sweep": place["sweep"] + 1},
            device_id_type=pl.DeviceIdType.MESH,
        )

    lane = lax.broadcasted_iota(jnp.int32, (cells, LANES), 1)
    leaving = lane >= OUT
    flat = traces.reshape(planes * (ny + 2) * nz_all, LANES)

    def rim_rows(plane, z):
        return pl.ds((plane * (ny + 2) + 1) * nz_all + z, ny, stride=nz_all)

    def send_sides(repeat):
        side = [
            jnp.concatenate([traces[p, ny, pad : pad + nz, :] for p in range(planes)], axis=0),
            jnp.concatenate([traces[p, 1, pad : pad + nz, :] for p in range(planes)], axis=0),
            jnp.concatenate([flat[rim_rows(p, pad + nz - 1), :] for p in range(planes)], axis=0),
            jnp.concatenate([flat[rim_rows(p, pad), :] for p in range(planes)], axis=0),
        ]
        for face, axis, step in faces:
            side_out[repeat, face, 0 : side[face].shape[0] // 4, :] = packed(side[face], face * WIDTH)
        for face, axis, step in faces:

            @pl.when(has(axis, step))
            def _(face=face, axis=axis, step=step):
                side_copy(repeat, face, axis, step).start()

    def take_sides(repeat):
        for face, axis, step in faces:

            @pl.when(has(axis, -step))
            def _(face=face, axis=axis, step=step):
                side_copy(repeat, face, axis, step).wait_recv()
                count = planes * (nz if axis == "cross" else ny)
                rows = unpacked(side_in[repeat, face, 0 : count // 4, :], face * WIDTH)
                for p in range(planes):
                    if axis == "cross":
                        piece = rows[p * nz : (p + 1) * nz]
                        traces[p, 0 if step > 0 else ny + 1, pad : pad + nz, :] = piece
                    else:
                        piece = rows[p * ny : (p + 1) * ny]
                        flat[rim_rows(p, pad - 1 if step > 0 else pad + nz), :] = piece

    maps = jnp.concatenate([extract[k] for k in range(4)], axis=1)
    w_extract[...] = doubled(maps)
    traces[:, 0, :, :] = jnp.zeros((planes, nz_all, LANES), f32)
    traces[:, ny + 1, :, :] = jnp.zeros((planes, nz_all, LANES), f32)
    nothing = jnp.zeros((planes, ny, pad, LANES), f32)
    traces[:, 1 : ny + 1, 0:pad, :] = nothing
    traces[:, 1 : ny + 1, pad + nz : nz_all, :] = nothing
    guess_copy.wait()

    def guess_traces(p, _):
        rows = product(guess[p].reshape(cells, LANES), w_extract[...])
        traces[p, 1 : ny + 1, pad : pad + nz, :] = rows.reshape(ny, nz, LANES)
        return 0

    lax.fori_loop(0, planes, guess_traces, 0)
    pl.semaphore_wait(barrier, expected)
    send_sides(0)

    diag = inv_diag[...]
    w_diag[...] = doubled(diag)
    w_a[...] = doubled(exact(jnp.concatenate([face_mats[k] for k in (0, 1, 3, 4)], axis=0), diag))
    w_b[...] = doubled(exact(jnp.concatenate([face_mats[k] for k in (2, 2, 5, 5)], axis=0), diag))
    lift_full[...] = jnp.zeros((LANES, LANES), f32)
    lift_full[OUT:LANES, 0:OUT] = lift[...]
    full = lift_full[...]
    w_lift[...] = doubled(full)
    lift_extract = exact(full, maps)
    w_lift_extract[...] = doubled(lift_extract)
    w_ahead[...] = doubled(
        jnp.concatenate(
            [jnp.zeros((2 * WIDTH, LANES), f32), lift_extract[OUT:LANES], maps[OUT:LANES]], axis=0
        )
    )
    start[...] = jnp.zeros((cells, LANES), f32)
    start[:, 0:WIDTH] = boundary[...].reshape(cells, WIDTH)
    upwind = place["sweep"] == 0
    start[...] = jnp.where(jnp.logical_and(leaving, upwind), turned(start[...], OUT), 0.0)

    unit = (
        lax.broadcasted_iota(jnp.int32, (nz, nz), 0) == lax.broadcasted_iota(jnp.int32, (nz, nz), 1)
    ).astype(f32)
    ones = jnp.ones((nz, LANES), bf16)
    log_rows = jnp.log(jnp.concatenate([transport[...]] * 4, axis=1))
    carried[0] = jnp.where(leaving, 1.0, 0.0)
    ahead_lanes = jnp.logical_and(lane >= OUT - WIDTH, lane < OUT)
    rhs_copy.wait()
    for p in range(planes):
        code = (scale[p] + 4 * wind[0, p] + 8 * wind[1, p]).astype(f32)
        spread = (code[:, None, :] * unit[None]).reshape(cells, nz).astype(bf16)
        code = jnp.dot(spread, ones, preferred_element_type=f32)
        wind_z = code >= 7.5
        code = jnp.where(wind_z, code - 8.0, code)
        wind_y = code >= 3.5
        index = jnp.where(wind_y, code - 4.0, code)
        wind_y = wind_y.astype(f32)
        wind_z = wind_z.astype(f32)
        kappa = 0.5 + 0.25 * index
        inverse = 1.0 / (1.0 + kappa)
        mask[p] = jnp.where(
            lane < WIDTH,
            wind_y,
            jnp.where(lane < 2 * WIDTH, 1.0 - wind_y, jnp.where(lane < OUT, wind_z, 1.0 - wind_z)),
        )
        gain_a[p] = kappa * inverse
        gain_b[p] = inverse
        scaled_rhs[p] = inverse * product(rhs[p].reshape(cells, LANES), w_diag[...])
        factor = jnp.where(leaving, jnp.exp(kappa * log_rows[p : p + 1]), 0.0)
        through[p] = factor
        now = carried[p]
        later = factor * now
        ahead[p] = jnp.where(ahead_lanes, turned(now, -WIDTH), later)
        carried[p + 1] = later
    relay_gain[...] = packed(carried[planes], OUT)

    for repeat in range(SWEEPS):
        final = repeat == SWEEPS - 1
        take_sides(repeat)
        sums[0] = start[...]

        def base_plane(p, _):
            below = traces[p, 0:ny, pad : pad + nz, :].reshape(cells, LANES)
            above = traces[p, 2 : ny + 2, pad : pad + nz, :].reshape(cells, LANES)
            left = traces[p, 1 : ny + 1, pad - 1 : pad - 1 + nz, :].reshape(cells, LANES)
            right = traces[p, 1 : ny + 1, pad + 1 : pad + 1 + nz, :].reshape(cells, LANES)
            near = jnp.where(
                lane < WIDTH,
                below,
                jnp.where(lane < 2 * WIDTH, above, jnp.where(lane < OUT, left, right)),
            )
            by_a = product(near, w_a[...])
            by_b = product(mask[p] * near, w_b[...])
            value = scaled_rhs[p] - gain_a[p] * by_a - gain_b[p] * by_b
            base[p] = value
            sums[p + 1] = through[p] * sums[p] + jnp.where(leaving, value, 0.0)
            return 0

        lax.fori_loop(0, planes, base_plane, 0)
        relay_sum[...] = packed(sums[planes], OUT)

        @pl.when(upwind)
        def _():
            relay_out[repeat] = relay_sum[...]

            @pl.when(last["sweep"] > 0)
            def _():
                relay_copy(repeat).start()

        if not final:

            def local_traces(p, _):
                inner = sums[p]
                value = base[p] + through[p] * inner
                rows = product(value, w_extract[...]) + product(inner, w_lift_extract[...])
                traces[p, 1 : ny + 1, pad : pad + nz, :] = rows.reshape(ny, nz, LANES)
                return 0

            lax.fori_loop(0, planes, local_traces, 0)

        @pl.when(jnp.logical_not(upwind))
        def _():
            relay_copy(repeat).wait_recv()
            arrived = relay_in[repeat]
            relay_out[repeat] = relay_gain[...] * arrived + relay_sum[...]

            @pl.when(place["sweep"] < last["sweep"])
            def _():
                relay_copy(repeat).start()

            here = jnp.where(leaving, unpacked(arrived, OUT), 0.0)
            if final:

                def add_inflow(p, _):
                    sums[p] = sums[p] + carried[p] * here
                    return 0

                lax.fori_loop(0, planes, add_inflow, 0)
            else:
                start_pair[...] = here + turned(here, -WIDTH)

                def add_traces(p, _):
                    rows = product(ahead[p] * start_pair[...], w_ahead[...])
                    traces[p, 1 : ny + 1, pad : pad + nz, :] += rows.reshape(ny, nz, LANES)
                    return 0

                lax.fori_loop(0, planes, add_traces, 0)

        if not final:
            send_sides(repeat + 1)

    for p in range(planes):
        inner = sums[p]
        value = base[p] + through[p] * inner + product(inner, w_lift[...])
        rhs[p] = value.reshape(ny, nz, LANES)
        pltpu.make_async_copy(rhs.at[p], out_hbm.at[p], store_sem.at[p]).start()
    for p in range(planes):
        pltpu.make_async_copy(rhs.at[p], out_hbm.at[p], store_sem.at[p]).wait()

    for repeat in range(SWEEPS):
        for face, axis, step in faces:

            @pl.when(has(axis, step))
            def _(face=face, axis=axis, step=step):
                side_copy(repeat, face, axis, step).wait_send()

        @pl.when(place["sweep"] < last["sweep"])
        def _():
            relay_copy(repeat).wait_send()


def per_device(
    rhs, guess, inv_diag, face_mats, extract, lift, transport, boundary, scale_index, wind
):
    planes, ny, nz, _ = rhs.shape
    cells = ny * nz
    whole = pl.BlockSpec(memory_space=pltpu.VMEM)
    anywhere = pl.BlockSpec(memory_space=pl.ANY)
    field = pltpu.VMEM((planes, ny, nz, LANES), f32)
    rows = pltpu.VMEM((planes, cells, LANES), f32)
    rows_more = pltpu.VMEM((planes + 1, cells, LANES), f32)
    weight = pltpu.VMEM((2 * LANES, 2 * LANES), bf16)
    plane = pltpu.VMEM((cells, LANES), f32)
    relay = pltpu.VMEM((cells // 4, LANES), f32)
    rim = planes * max(ny, nz) // 4
    return pl.pallas_call(
        kernel,
        out_shape=jax.ShapeDtypeStruct(rhs.shape, f32),
        in_specs=[anywhere] * 2 + [whole] * 8,
        out_specs=anywhere,
        scratch_shapes=[
            field, field, pltpu.VMEM((planes, ny + 2, nz + 16, LANES), f32),
            rows, rows, rows, rows, rows, rows_more, rows, rows, rows_more,
            weight, weight, weight, weight, weight, weight, weight,
            pltpu.VMEM((LANES, LANES), f32), relay, relay,
            plane, plane,
            pltpu.VMEM((SWEEPS, 4, rim, LANES), f32),
            pltpu.VMEM((SWEEPS, 4, rim, LANES), f32),
            pltpu.VMEM((SWEEPS, cells // 4, LANES), f32),
            pltpu.VMEM((SWEEPS, cells // 4, LANES), f32),
            pltpu.SemaphoreType.DMA((2,)),
            pltpu.SemaphoreType.DMA((planes,)),
            pltpu.SemaphoreType.DMA((SWEEPS, 4)),
            pltpu.SemaphoreType.DMA((SWEEPS, 4)),
            pltpu.SemaphoreType.DMA((SWEEPS,)),
            pltpu.SemaphoreType.DMA((SWEEPS,)),
        ],
        compiler_params=pltpu.CompilerParams(
            collective_id=0, has_side_effects=True, vmem_limit_bytes=56 * 2**20
        ),
    )(rhs, guess, inv_diag, face_mats, extract, lift, transport, boundary, scale_index, wind)


def solution(mesh):
    return jax.shard_map(
        per_device,
        mesh=mesh,
        in_specs=(
            P("sweep", "cross", "third", None),
            P("sweep", "cross", "third", None),
            P(),
            P(),
            P(),
            P(),
            P("sweep", None),
            P("cross", "third", None),
            P("sweep", "cross", "third"),
            P(None, "sweep", "cross", "third"),
        ),
        out_specs=P("sweep", "cross", "third", None),
        check_vma=False,
    )
```

```python
import functools

import jax
import jax.numpy as jnp
from jax import lax
from jax.experimental import pallas as pl
from jax.experimental.pallas import tpu as pltpu
from jax.sharding import PartitionSpec as P

SWEEPS = 2
LANES = 128
WIDTH = 32
OUT = LANES - WIDTH
f32 = jnp.float32
bf16 = jnp.bfloat16


def halves(value):
    high = value.astype(bf16)
    low = (value - high.astype(f32)).astype(bf16)
    return high, low


def doubled(weight):
    row = jnp.concatenate(halves(weight), axis=1)
    return jnp.concatenate([row, row], axis=0)


def product(left, weight):
    wide = jnp.concatenate(halves(left), axis=1)
    both = jnp.dot(wide, weight, preferred_element_type=f32)
    return both[:, :LANES] + both[:, LANES:]


def exact(left, right):
    return jnp.dot(left, right, precision=lax.Precision.HIGHEST, preferred_element_type=f32)


def turned(value, lanes):
    lanes = lanes % LANES
    return value if lanes == 0 else pltpu.roll(value, lanes, 1)


def packed(value, first):
    rows = value.shape[0] // 4
    lane = lax.broadcasted_iota(jnp.int32, (rows, LANES), 1)
    out = None
    for group in range(4):
        piece = turned(value[group * rows : (group + 1) * rows], group * WIDTH - first)
        out = piece if out is None else jnp.where(lane >= group * WIDTH, piece, out)
    return out


def unpacked(value, first):
    return jnp.concatenate([turned(value, first - group * WIDTH) for group in range(4)], axis=0)


def kernel(*refs):
    sources, out, refs = refs[:10], refs[10], refs[11:]
    held, refs = refs[:10], refs[10:]
    rhs, guess, inv_diag, face_mats, extract, lift, transport, boundary, scale, wind = held
    (
        traces, scaled_rhs, gain_a, gain_b, mask, through, carried, ahead, base, sums,
        w_extract, w_diag, w_a, w_b, w_lift, w_lift_extract, w_ahead, lift_full, relay_gain,
        relay_sum, start, start_pair, side_out, side_in, relay_out, relay_in,
        load_sem, side_send, side_recv, relay_send, relay_recv,
    ) = refs
    planes, ny, nz, _ = rhs.shape
    cells = ny * nz
    pad = 8
    nz_all = nz + 2 * pad
    place = {axis: lax.axis_index(axis) for axis in ("sweep", "cross", "third")}
    last = {axis: lax.axis_size(axis) - 1 for axis in place}

    loads = [
        pltpu.make_async_copy(source, target, load_sem.at[number])
        for number, (source, target) in enumerate(zip(sources, held))
    ]
    for number in (4, 1, 2, 3, 5, 8, 9, 6, 7, 0):
        loads[number].start()

    barrier = pltpu.get_barrier_semaphore()
    around = []
    for axis in place:
        around.append((axis, 1, place[axis] < last[axis]))
        around.append((axis, -1, place[axis] > 0))
    expected = jnp.int32(0)
    for axis, step, there in around:
        expected = expected + there.astype(jnp.int32)

        @pl.when(there)
        def _(axis=axis, step=step):
            pl.semaphore_signal(
                barrier, inc=1, device_id={axis: place[axis] + step},
                device_id_type=pl.DeviceIdType.MESH,
            )

    faces = ((0, "cross", 1), (1, "cross", -1), (2, "third", 1), (3, "third", -1))

    def has(axis, step):
        return place[axis] < last[axis] if step > 0 else place[axis] > 0

    def side_copy(repeat, face, axis, step):
        return pltpu.make_async_remote_copy(
            src_ref=side_out.at[repeat, face],
            dst_ref=side_in.at[repeat, face],
            send_sem=side_send.at[repeat, face],
            recv_sem=side_recv.at[repeat, face],
            device_id={axis: place[axis] + step},
            device_id_type=pl.DeviceIdType.MESH,
        )

    def relay_copy(repeat):
        return pltpu.make_async_remote_copy(
            src_ref=relay_out.at[repeat],
            dst_ref=relay_in.at[repeat],
            send_sem=relay_send.at[repeat],
            recv_sem=relay_recv.at[repeat],
            device_id={"sweep": place["sweep"] + 1},
            device_id_type=pl.DeviceIdType.MESH,
        )

    lane = lax.broadcasted_iota(jnp.int32, (cells, LANES), 1)
    leaving = lane >= OUT
    flat = traces.reshape(planes * (ny + 2) * nz_all, LANES)

    def rim_rows(plane, z):
        return pl.ds((plane * (ny + 2) + 1) * nz_all + z, ny, stride=nz_all)

    def send_sides(repeat):
        side = [
            jnp.concatenate([traces[p, ny, pad : pad + nz, :] for p in range(planes)], axis=0),
            jnp.concatenate([traces[p, 1, pad : pad + nz, :] for p in range(planes)], axis=0),
            jnp.concatenate([flat[rim_rows(p, pad + nz - 1), :] for p in range(planes)], axis=0),
            jnp.concatenate([flat[rim_rows(p, pad), :] for p in range(planes)], axis=0),
        ]
        for face, axis, step in faces:
            side_out[repeat, face, 0 : side[face].shape[0] // 4, :] = packed(side[face], face * WIDTH)
        for face, axis, step in faces:

            @pl.when(has(axis, step))
            def _(face=face, axis=axis, step=step):
                side_copy(repeat, face, axis, step).start()

    def take_sides(repeat):
        for face, axis, step in faces:

            @pl.when(has(axis, -step))
            def _(face=face, axis=axis, step=step):
                side_copy(repeat, face, axis, step).wait_recv()
                count = planes * (nz if axis == "cross" else ny)
                rows = unpacked(side_in[repeat, face, 0 : count // 4, :], face * WIDTH)
                for p in range(planes):
                    if axis == "cross":
                        piece = rows[p * nz : (p + 1) * nz]
                        traces[p, 0 if step > 0 else ny + 1, pad : pad + nz, :] = piece
                    else:
                        piece = rows[p * ny : (p + 1) * ny]
                        flat[rim_rows(p, pad - 1 if step > 0 else pad + nz), :] = piece

    loads[4].wait()
    maps = extract[...].reshape(LANES, LANES).T
    w_extract[...] = doubled(maps)
    traces[:, 0, :, :] = jnp.zeros((planes, nz_all, LANES), f32)
    traces[:, ny + 1, :, :] = jnp.zeros((planes, nz_all, LANES), f32)
    nothing = jnp.zeros((planes, ny, pad, LANES), f32)
    traces[:, 1 : ny + 1, 0:pad, :] = nothing
    traces[:, 1 : ny + 1, pad + nz : nz_all, :] = nothing
    loads[1].wait()

    def guess_traces(p, _):
        rows = product(guess[p].reshape(cells, LANES), w_extract[...])
        traces[p, 1 : ny + 1, pad : pad + nz, :] = rows.reshape(ny, nz, LANES)
        return 0

    lax.fori_loop(0, planes, guess_traces, 0)
    pl.semaphore_wait(barrier, expected)
    send_sides(0)

    for number in (2, 3, 5, 8, 9, 6, 7):
        loads[number].wait()
    diag = inv_diag[...]
    w_diag[...] = doubled(diag)
    w_a[...] = doubled(exact(jnp.concatenate([face_mats[k] for k in (0, 1, 3, 4)], axis=0), diag))
    w_b[...] = doubled(exact(jnp.concatenate([face_mats[k] for k in (2, 2, 5, 5)], axis=0), diag))
    lift_full[...] = jnp.zeros((LANES, LANES), f32)
    lift_full[OUT:LANES, 0:OUT] = lift[...]
    full = lift_full[...]
    w_lift[...] = doubled(full)
    lift_extract = exact(full, maps)
    w_lift_extract[...] = doubled(lift_extract)
    w_ahead[...] = doubled(
        jnp.concatenate(
            [jnp.zeros((2 * WIDTH, LANES), f32), lift_extract[OUT:LANES], maps[OUT:LANES]], axis=0
        )
    )
    start[...] = jnp.zeros((cells, LANES), f32)
    start[:, 0:WIDTH] = boundary[...].reshape(cells, WIDTH)
    upwind = place["sweep"] == 0
    start[...] = jnp.where(jnp.logical_and(leaving, upwind), turned(start[...], OUT), 0.0)

    unit = (
        lax.broadcasted_iota(jnp.int32, (nz, nz), 0) == lax.broadcasted_iota(jnp.int32, (nz, nz), 1)
    ).astype(f32)
    ones = jnp.ones((nz, LANES), bf16)
    log_rows = jnp.log(jnp.concatenate([transport[...]] * 4, axis=1))
    carried[0] = jnp.where(leaving, 1.0, 0.0)
    ahead_lanes = jnp.logical_and(lane >= OUT - WIDTH, lane < OUT)
    loads[0].wait()
    for p in range(planes):
        code = (scale[p] + 4 * wind[0, p] + 8 * wind[1, p]).astype(f32)
        spread = (code[:, None, :] * unit[None]).reshape(cells, nz).astype(bf16)
        code = jnp.dot(spread, ones, preferred_element_type=f32)
        wind_z = code >= 7.5
        code = jnp.where(wind_z, code - 8.0, code)
        wind_y = code >= 3.5
        index = jnp.where(wind_y, code - 4.0, code)
        wind_y = wind_y.astype(f32)
        wind_z = wind_z.astype(f32)
        kappa = 0.5 + 0.25 * index
        inverse = 1.0 / (1.0 + kappa)
        mask[p] = jnp.where(
            lane < WIDTH,
            wind_y,
            jnp.where(lane < 2 * WIDTH, 1.0 - wind_y, jnp.where(lane < OUT, wind_z, 1.0 - wind_z)),
        )
        gain_a[p] = kappa * inverse
        gain_b[p] = inverse
        scaled_rhs[p] = inverse * product(rhs[p].reshape(cells, LANES), w_diag[...])
        factor = jnp.where(leaving, jnp.exp(kappa * log_rows[p : p + 1]), 0.0)
        through[p] = factor
        now = carried[p]
        later = factor * now
        ahead[p] = jnp.where(ahead_lanes, turned(now, -WIDTH), later)
        carried[p + 1] = later
    relay_gain[...] = packed(carried[planes], OUT)

    for repeat in range(SWEEPS):
        final = repeat == SWEEPS - 1
        take_sides(repeat)
        sums[0] = start[...]

        def base_plane(p, _):
            below = traces[p, 0:ny, pad : pad + nz, :].reshape(cells, LANES)
            above = traces[p, 2 : ny + 2, pad : pad + nz, :].reshape(cells, LANES)
            left = traces[p, 1 : ny + 1, pad - 1 : pad - 1 + nz, :].reshape(cells, LANES)
            right = traces[p, 1 : ny + 1, pad + 1 : pad + 1 + nz, :].reshape(cells, LANES)
            near = jnp.where(
                lane < WIDTH,
                below,
                jnp.where(lane < 2 * WIDTH, above, jnp.where(lane < OUT, left, right)),
            )
            by_a = product(near, w_a[...])
            by_b = product(mask[p] * near, w_b[...])
            value = scaled_rhs[p] - gain_a[p] * by_a - gain_b[p] * by_b
            base[p] = value
            sums[p + 1] = through[p] * sums[p] + jnp.where(leaving, value, 0.0)
            return 0

        lax.fori_loop(0, planes, base_plane, 0)
        relay_sum[...] = packed(sums[planes], OUT)

        @pl.when(upwind)
        def _():
            relay_out[repeat] = relay_sum[...]

            @pl.when(last["sweep"] > 0)
            def _():
                relay_copy(repeat).start()

        if not final:

            def local_traces(p, _):
                inner = sums[p]
                value = base[p] + through[p] * inner
                rows = product(value, w_extract[...]) + product(inner, w_lift_extract[...])
                traces[p, 1 : ny + 1, pad : pad + nz, :] = rows.reshape(ny, nz, LANES)
                return 0

            lax.fori_loop(0, planes, local_traces, 0)

        @pl.when(jnp.logical_not(upwind))
        def _():
            relay_copy(repeat).wait_recv()
            arrived = relay_in[repeat]
            relay_out[repeat] = relay_gain[...] * arrived + relay_sum[...]

            @pl.when(place["sweep"] < last["sweep"])
            def _():
                relay_copy(repeat).start()

            here = jnp.where(leaving, unpacked(arrived, OUT), 0.0)
            if final:

                def add_inflow(p, _):
                    sums[p] = sums[p] + carried[p] * here
                    return 0

                lax.fori_loop(0, planes, add_inflow, 0)
            else:
                start_pair[...] = here + turned(here, -WIDTH)

                def add_traces(p, _):
                    rows = product(ahead[p] * start_pair[...], w_ahead[...])
                    traces[p, 1 : ny + 1, pad : pad + nz, :] += rows.reshape(ny, nz, LANES)
                    return 0

                lax.fori_loop(0, planes, add_traces, 0)

        if not final:
            send_sides(repeat + 1)

    for p in range(planes):
        inner = sums[p]
        value = base[p] + through[p] * inner + product(inner, w_lift[...])
        out[p] = value.reshape(ny, nz, LANES)

    for repeat in range(SWEEPS):
        for face, axis, step in faces:

            @pl.when(has(axis, step))
            def _(face=face, axis=axis, step=step):
                side_copy(repeat, face, axis, step).wait_send()

        @pl.when(place["sweep"] < last["sweep"])
        def _():
            relay_copy(repeat).wait_send()


def per_device(
    rhs, guess, inv_diag, face_mats, extract, lift, transport, boundary, scale_index, wind
):
    planes, ny, nz, _ = rhs.shape
    cells = ny * nz
    turned_extract = extract.transpose(0, 2, 1)
    whole = pl.BlockSpec(memory_space=pltpu.VMEM)
    far = pl.BlockSpec(memory_space=pltpu.HBM)
    field = pltpu.VMEM((planes, ny, nz, LANES), f32)
    rows = pltpu.VMEM((planes, cells, LANES), f32)
    rows_more = pltpu.VMEM((planes + 1, cells, LANES), f32)
    weight = pltpu.VMEM((2 * LANES, 2 * LANES), bf16)
    plane = pltpu.VMEM((cells, LANES), f32)
    relay = pltpu.VMEM((cells // 4, LANES), f32)
    rim = planes * max(ny, nz) // 4
    return pl.pallas_call(
        kernel,
        out_shape=jax.ShapeDtypeStruct(rhs.shape, f32),
        in_specs=[far] * 10,
        out_specs=whole,
        scratch_shapes=[
            field, field, pltpu.VMEM(inv_diag.shape, f32), pltpu.VMEM(face_mats.shape, f32),
            pltpu.VMEM(turned_extract.shape, f32), pltpu.VMEM(lift.shape, f32),
            pltpu.VMEM(transport.shape, f32), pltpu.VMEM(boundary.shape, f32),
            pltpu.VMEM(scale_index.shape, jnp.int32), pltpu.VMEM(wind.shape, jnp.int32),
            pltpu.VMEM((planes, ny + 2, nz + 16, LANES), f32),
            rows, rows, rows, rows, rows, rows_more, rows, rows, rows_more,
            weight, weight, weight, weight, weight, weight, weight,
            pltpu.VMEM((LANES, LANES), f32), relay, relay,
            plane, plane,
            pltpu.VMEM((SWEEPS, 4, rim, LANES), f32),
            pltpu.VMEM((SWEEPS, 4, rim, LANES), f32),
            pltpu.VMEM((SWEEPS, cells // 4, LANES), f32),
            pltpu.VMEM((SWEEPS, cells // 4, LANES), f32),
            pltpu.SemaphoreType.DMA((10,)),
            pltpu.SemaphoreType.DMA((SWEEPS, 4)),
            pltpu.SemaphoreType.DMA((SWEEPS, 4)),
            pltpu.SemaphoreType.DMA((SWEEPS,)),
            pltpu.SemaphoreType.DMA((SWEEPS,)),
        ],
        compiler_params=pltpu.CompilerParams(
            collective_id=0, has_side_effects=True, vmem_limit_bytes=24 * 2**20
        ),
    )(
        *(
            pltpu.with_memory_space_constraint(operand, pltpu.HBM)
            for operand in (
                rhs, guess, inv_diag, face_mats, turned_extract, lift, transport, boundary,
                scale_index, wind,
            )
        )
    )


def solution(mesh):
    return jax.shard_map(
        per_device,
        mesh=mesh,
        in_specs=(
            P("sweep", "cross", "third", None),
            P("sweep", "cross", "third", None),
            P(),
            P(),
            P(),
            P(),
            P("sweep", None),
            P("cross", "third", None),
            P("sweep", "cross", "third"),
            P(None, "sweep", "cross", "third"),
        ),
        out_specs=P("sweep", "cross", "third", None),
        check_vma=False,
    )
```

```python
import functools

import jax
import jax.numpy as jnp
from jax import lax
from jax.experimental import pallas as pl
from jax.experimental.pallas import tpu as pltpu
from jax.sharding import PartitionSpec as P

SWEEPS = 2
LANES = 128
WIDTH = 32
PIECES = 4
OUT = LANES - WIDTH
f32 = jnp.float32
bf16 = jnp.bfloat16


def halves(value):
    high = value.astype(bf16)
    low = (value - high.astype(f32)).astype(bf16)
    return high, low


def doubled(weight):
    row = jnp.concatenate(halves(weight), axis=1)
    return jnp.concatenate([row, row], axis=0)


def product(left, weight):
    wide = jnp.concatenate(halves(left), axis=1)
    both = jnp.dot(wide, weight, preferred_element_type=f32)
    return both[:, :LANES] + both[:, LANES:]


def exact(left, right):
    return jnp.dot(left, right, precision=lax.Precision.HIGHEST, preferred_element_type=f32)


def turned(value, lanes):
    lanes = lanes % LANES
    return value if lanes == 0 else pltpu.roll(value, lanes, 1)


def packed(value, first):
    rows = value.shape[0] // 4
    lane = lax.broadcasted_iota(jnp.int32, (rows, LANES), 1)
    out = None
    for group in range(4):
        piece = turned(value[group * rows : (group + 1) * rows], group * WIDTH - first)
        out = piece if out is None else jnp.where(lane >= group * WIDTH, piece, out)
    return out


def unpacked(value, first):
    return jnp.concatenate([turned(value, first - group * WIDTH) for group in range(4)], axis=0)


def kernel(*refs):
    sources, out, refs = refs[:10], refs[10], refs[11:]
    held, refs = refs[:10], refs[10:]
    rhs, guess, inv_diag, face_mats, extract, lift, transport, boundary, scale, wind = held
    (
        traces, scaled_rhs, gain_a, gain_b, mask, through, carried, ahead, base, sums,
        w_extract, w_diag, w_a, w_b, w_lift, w_lift_extract, w_ahead, lift_full, relay_gain,
        relay_sum, start, start_pair, side_out, side_in, relay_out, relay_in,
        load_sem, side_send, side_recv, relay_send, relay_recv,
    ) = refs
    planes, ny, nz, _ = rhs.shape
    cells = ny * nz
    pad = 8
    nz_all = nz + 2 * pad
    place = {axis: lax.axis_index(axis) for axis in ("sweep", "cross", "third")}
    last = {axis: lax.axis_size(axis) - 1 for axis in place}

    loads = [
        pltpu.make_async_copy(source, target, load_sem.at[number])
        for number, (source, target) in enumerate(zip(sources, held))
    ]
    for number in (4, 1, 2, 3, 5, 8, 9, 6, 7, 0):
        loads[number].start()

    barrier = pltpu.get_barrier_semaphore()
    around = []
    for axis in place:
        around.append((axis, 1, place[axis] < last[axis]))
        around.append((axis, -1, place[axis] > 0))
    expected = jnp.int32(0)
    for axis, step, there in around:
        expected = expected + there.astype(jnp.int32)

        @pl.when(there)
        def _(axis=axis, step=step):
            pl.semaphore_signal(
                barrier, inc=1, device_id={axis: place[axis] + step},
                device_id_type=pl.DeviceIdType.MESH,
            )

    faces = ((0, "cross", 1), (1, "cross", -1), (2, "third", 1), (3, "third", -1))

    def has(axis, step):
        return place[axis] < last[axis] if step > 0 else place[axis] > 0

    def side_copy(repeat, face, axis, step):
        return pltpu.make_async_remote_copy(
            src_ref=side_out.at[repeat, face],
            dst_ref=side_in.at[repeat, face],
            send_sem=side_send.at[repeat, face],
            recv_sem=side_recv.at[repeat, face],
            device_id={axis: place[axis] + step},
            device_id_type=pl.DeviceIdType.MESH,
        )

    relay_rows = cells // 4 // PIECES

    def relay_copy(repeat, piece):
        return pltpu.make_async_remote_copy(
            src_ref=relay_out.at[repeat, piece],
            dst_ref=relay_in.at[repeat, piece],
            send_sem=relay_send.at[repeat, piece],
            recv_sem=relay_recv.at[repeat, piece],
            device_id={"sweep": place["sweep"] + 1},
            device_id_type=pl.DeviceIdType.MESH,
        )

    lane = lax.broadcasted_iota(jnp.int32, (cells, LANES), 1)
    leaving = lane >= OUT
    flat = traces.reshape(planes * (ny + 2) * nz_all, LANES)

    def rim_rows(plane, z):
        return pl.ds((plane * (ny + 2) + 1) * nz_all + z, ny, stride=nz_all)

    def send_sides(repeat):
        side = [
            jnp.concatenate([traces[p, ny, pad : pad + nz, :] for p in range(planes)], axis=0),
            jnp.concatenate([traces[p, 1, pad : pad + nz, :] for p in range(planes)], axis=0),
            jnp.concatenate([flat[rim_rows(p, pad + nz - 1), :] for p in range(planes)], axis=0),
            jnp.concatenate([flat[rim_rows(p, pad), :] for p in range(planes)], axis=0),
        ]
        for face, axis, step in faces:
            side_out[repeat, face, 0 : side[face].shape[0] // 4, :] = packed(side[face], face * WIDTH)
        for face, axis, step in faces:

            @pl.when(has(axis, step))
            def _(face=face, axis=axis, step=step):
                side_copy(repeat, face, axis, step).start()

    def take_sides(repeat):
        for face, axis, step in faces:

            @pl.when(has(axis, -step))
            def _(face=face, axis=axis, step=step):
                side_copy(repeat, face, axis, step).wait_recv()
                count = planes * (nz if axis == "cross" else ny)
                rows = unpacked(side_in[repeat, face, 0 : count // 4, :], face * WIDTH)
                for p in range(planes):
                    if axis == "cross":
                        piece = rows[p * nz : (p + 1) * nz]
                        traces[p, 0 if step > 0 else ny + 1, pad : pad + nz, :] = piece
                    else:
                        piece = rows[p * ny : (p + 1) * ny]
                        flat[rim_rows(p, pad - 1 if step > 0 else pad + nz), :] = piece

    loads[4].wait()
    maps = extract[...].reshape(LANES, LANES).T
    w_extract[...] = doubled(maps)
    traces[:, 0, :, :] = jnp.zeros((planes, nz_all, LANES), f32)
    traces[:, ny + 1, :, :] = jnp.zeros((planes, nz_all, LANES), f32)
    nothing = jnp.zeros((planes, ny, pad, LANES), f32)
    traces[:, 1 : ny + 1, 0:pad, :] = nothing
    traces[:, 1 : ny + 1, pad + nz : nz_all, :] = nothing
    loads[1].wait()

    def guess_traces(p, _):
        rows = product(guess[p].reshape(cells, LANES), w_extract[...])
        traces[p, 1 : ny + 1, pad : pad + nz, :] = rows.reshape(ny, nz, LANES)
        return 0

    lax.fori_loop(0, planes, guess_traces, 0, unroll=4)
    pl.semaphore_wait(barrier, expected)
    send_sides(0)

    for number in (2, 3, 5, 8, 9, 6, 7):
        loads[number].wait()
    diag = inv_diag[...]
    w_diag[...] = doubled(diag)
    w_a[...] = doubled(exact(jnp.concatenate([face_mats[k] for k in (0, 1, 3, 4)], axis=0), diag))
    w_b[...] = doubled(exact(jnp.concatenate([face_mats[k] for k in (2, 2, 5, 5)], axis=0), diag))
    lift_full[...] = jnp.zeros((LANES, LANES), f32)
    lift_full[OUT:LANES, 0:OUT] = lift[...]
    full = lift_full[...]
    w_lift[...] = doubled(full)
    lift_extract = exact(full, maps)
    w_lift_extract[...] = doubled(lift_extract)
    w_ahead[...] = doubled(
        jnp.concatenate(
            [jnp.zeros((2 * WIDTH, LANES), f32), lift_extract[OUT:LANES], maps[OUT:LANES]], axis=0
        )
    )
    start[...] = jnp.zeros((cells, LANES), f32)
    start[:, 0:WIDTH] = boundary[...].reshape(cells, WIDTH)
    upwind = place["sweep"] == 0
    start[...] = jnp.where(jnp.logical_and(leaving, upwind), turned(start[...], OUT), 0.0)

    unit = (
        lax.broadcasted_iota(jnp.int32, (nz, nz), 0) == lax.broadcasted_iota(jnp.int32, (nz, nz), 1)
    ).astype(f32)
    ones = jnp.ones((nz, LANES), bf16)
    log_rows = jnp.log(jnp.concatenate([transport[...]] * 4, axis=1))
    carried[0] = jnp.where(leaving, 1.0, 0.0)
    ahead_lanes = jnp.logical_and(lane >= OUT - WIDTH, lane < OUT)
    loads[0].wait()
    for p in range(planes):
        code = (scale[p] + 4 * wind[0, p] + 8 * wind[1, p]).astype(f32)
        spread = (code[:, None, :] * unit[None]).reshape(cells, nz).astype(bf16)
        code = jnp.dot(spread, ones, preferred_element_type=f32)
        wind_z = code >= 7.5
        code = jnp.where(wind_z, code - 8.0, code)
        wind_y = code >= 3.5
        index = jnp.where(wind_y, code - 4.0, code)
        wind_y = wind_y.astype(f32)
        wind_z = wind_z.astype(f32)
        kappa = 0.5 + 0.25 * index
        inverse = 1.0 / (1.0 + kappa)
        mask[p] = jnp.where(
            lane < WIDTH,
            wind_y,
            jnp.where(lane < 2 * WIDTH, 1.0 - wind_y, jnp.where(lane < OUT, wind_z, 1.0 - wind_z)),
        )
        gain_a[p] = kappa * inverse
        gain_b[p] = inverse
        scaled_rhs[p] = inverse * product(rhs[p].reshape(cells, LANES), w_diag[...])
        factor = jnp.where(leaving, jnp.exp(kappa * log_rows[p : p + 1]), 0.0)
        through[p] = factor
        now = carried[p]
        later = factor * now
        ahead[p] = jnp.where(ahead_lanes, turned(now, -WIDTH), later)
        carried[p + 1] = later
    relay_gain[...] = packed(carried[planes], OUT)

    for repeat in range(SWEEPS):
        final = repeat == SWEEPS - 1
        take_sides(repeat)
        sums[0] = start[...]

        def base_plane(p, _):
            below = traces[p, 0:ny, pad : pad + nz, :].reshape(cells, LANES)
            above = traces[p, 2 : ny + 2, pad : pad + nz, :].reshape(cells, LANES)
            left = traces[p, 1 : ny + 1, pad - 1 : pad - 1 + nz, :].reshape(cells, LANES)
            right = traces[p, 1 : ny + 1, pad + 1 : pad + 1 + nz, :].reshape(cells, LANES)
            near = jnp.where(
                lane < WIDTH,
                below,
                jnp.where(lane < 2 * WIDTH, above, jnp.where(lane < OUT, left, right)),
            )
            by_a = product(near, w_a[...])
            by_b = product(mask[p] * near, w_b[...])
            value = scaled_rhs[p] - gain_a[p] * by_a - gain_b[p] * by_b
            base[p] = value
            sums[p + 1] = through[p] * sums[p] + jnp.where(leaving, value, 0.0)
            return 0

        lax.fori_loop(0, planes, base_plane, 0, unroll=4)
        relay_sum[...] = packed(sums[planes], OUT)

        @pl.when(upwind)
        def _():
            for piece in range(PIECES):
                relay_out[repeat, piece] = relay_sum[
                    piece * relay_rows : (piece + 1) * relay_rows, :
                ]

                @pl.when(last["sweep"] > 0)
                def _(piece=piece):
                    relay_copy(repeat, piece).start()

        if not final:

            def local_traces(p, _):
                inner = sums[p]
                value = base[p] + through[p] * inner
                rows = product(value, w_extract[...]) + product(inner, w_lift_extract[...])
                traces[p, 1 : ny + 1, pad : pad + nz, :] = rows.reshape(ny, nz, LANES)
                return 0

            lax.fori_loop(0, planes, local_traces, 0, unroll=4)

        @pl.when(jnp.logical_not(upwind))
        def _():
            for piece in range(PIECES):
                rows = slice(piece * relay_rows, (piece + 1) * relay_rows)
                relay_copy(repeat, piece).wait_recv()
                relay_out[repeat, piece] = (
                    relay_gain[rows, :] * relay_in[repeat, piece] + relay_sum[rows, :]
                )

                @pl.when(place["sweep"] < last["sweep"])
                def _(piece=piece):
                    relay_copy(repeat, piece).start()

            arrived = jnp.concatenate([relay_in[repeat, piece] for piece in range(PIECES)], axis=0)
            here = jnp.where(leaving, unpacked(arrived, OUT), 0.0)
            if final:

                def add_inflow(p, _):
                    sums[p] = sums[p] + carried[p] * here
                    return 0

                lax.fori_loop(0, planes, add_inflow, 0, unroll=4)
            else:
                start_pair[...] = here + turned(here, -WIDTH)

                def add_traces(p, _):
                    rows = product(ahead[p] * start_pair[...], w_ahead[...])
                    traces[p, 1 : ny + 1, pad : pad + nz, :] += rows.reshape(ny, nz, LANES)
                    return 0

                lax.fori_loop(0, planes, add_traces, 0, unroll=4)

        if not final:
            send_sides(repeat + 1)

    for p in range(planes):
        inner = sums[p]
        value = base[p] + through[p] * inner + product(inner, w_lift[...])
        out[p] = value.reshape(ny, nz, LANES)

    for repeat in range(SWEEPS):
        for face, axis, step in faces:

            @pl.when(has(axis, step))
            def _(face=face, axis=axis, step=step):
                side_copy(repeat, face, axis, step).wait_send()

        @pl.when(place["sweep"] < last["sweep"])
        def _():
            for piece in range(PIECES):
                relay_copy(repeat, piece).wait_send()


def per_device(
    rhs, guess, inv_diag, face_mats, extract, lift, transport, boundary, scale_index, wind
):
    planes, ny, nz, _ = rhs.shape
    cells = ny * nz
    turned_extract = extract.transpose(0, 2, 1)
    whole = pl.BlockSpec(memory_space=pltpu.VMEM)
    far = pl.BlockSpec(memory_space=pltpu.HBM)
    field = pltpu.VMEM((planes, ny, nz, LANES), f32)
    rows = pltpu.VMEM((planes, cells, LANES), f32)
    rows_more = pltpu.VMEM((planes + 1, cells, LANES), f32)
    weight = pltpu.VMEM((2 * LANES, 2 * LANES), bf16)
    plane = pltpu.VMEM((cells, LANES), f32)
    relay = pltpu.VMEM((cells // 4, LANES), f32)
    rim = planes * max(ny, nz) // 4
    return pl.pallas_call(
        kernel,
        out_shape=jax.ShapeDtypeStruct(rhs.shape, f32),
        in_specs=[far] * 10,
        out_specs=whole,
        scratch_shapes=[
            field, field, pltpu.VMEM(inv_diag.shape, f32), pltpu.VMEM(face_mats.shape, f32),
            pltpu.VMEM(turned_extract.shape, f32), pltpu.VMEM(lift.shape, f32),
            pltpu.VMEM(transport.shape, f32), pltpu.VMEM(boundary.shape, f32),
            pltpu.VMEM(scale_index.shape, jnp.int32), pltpu.VMEM(wind.shape, jnp.int32),
            pltpu.VMEM((planes, ny + 2, nz + 16, LANES), f32),
            rows, rows, rows, rows, rows, rows_more, rows, rows, rows_more,
            weight, weight, weight, weight, weight, weight, weight,
            pltpu.VMEM((LANES, LANES), f32), relay, relay,
            plane, plane,
            pltpu.VMEM((SWEEPS, 4, rim, LANES), f32),
            pltpu.VMEM((SWEEPS, 4, rim, LANES), f32),
            pltpu.VMEM((SWEEPS, PIECES, cells // 4 // PIECES, LANES), f32),
            pltpu.VMEM((SWEEPS, PIECES, cells // 4 // PIECES, LANES), f32),
            pltpu.SemaphoreType.DMA((10,)),
            pltpu.SemaphoreType.DMA((SWEEPS, 4)),
            pltpu.SemaphoreType.DMA((SWEEPS, 4)),
            pltpu.SemaphoreType.DMA((SWEEPS, PIECES)),
            pltpu.SemaphoreType.DMA((SWEEPS, PIECES)),
        ],
        compiler_params=pltpu.CompilerParams(
            collective_id=0, has_side_effects=True, vmem_limit_bytes=24 * 2**20
        ),
    )(
        *(
            pltpu.with_memory_space_constraint(operand, pltpu.HBM)
            for operand in (
                rhs, guess, inv_diag, face_mats, turned_extract, lift, transport, boundary,
                scale_index, wind,
            )
        )
    )


def solution(mesh):
    return jax.shard_map(
        per_device,
        mesh=mesh,
        in_specs=(
            P("sweep", "cross", "third", None),
            P("sweep", "cross", "third", None),
            P(),
            P(),
            P(),
            P(),
            P("sweep", None),
            P("cross", "third", None),
            P("sweep", "cross", "third"),
            P(None, "sweep", "cross", "third"),
        ),
        out_specs=P("sweep", "cross", "third", None),
        check_vma=False,
    )
```
